256 devices in a mesh: depth: 4 (over x), row: 16 (over z, y_hi), col: 4 (over y_lo, core).
Axes of the slice: x: 4, y: 4 (y_hi: 2, y_lo: 2; y = y_hi * 2 + y_lo), z: 8, core: 2. Of those that a mesh axis runs over, the one named last changes fastest.
Arguments:
- tokens: bfloat16 [768, 8192], P(('depth', 'row')), may hold values from -6 to 6
- out_grad: bfloat16 [768, 8192], P(('depth', 'row')), may hold values from -0.59765625 to 0.59765625
- gate_weight: bfloat16 [8192, 16384], P('depth', ('row', 'col')), may hold values from -0.0625 to 0.0625
- up_weight: bfloat16 [8192, 16384], P('depth', ('row', 'col')), may hold values from -0.0625 to 0.0625
- down_weight: bfloat16 [16384, 8192], P(('row', 'col'), 'depth'), may hold values from -0.046875 to 0.046875
Outputs:
- input_grad: bfloat16 [768, 8192], P(('depth', 'row', 'col'))
- gate_grad: bfloat16 [8192, 16384], P('depth', ('row', 'col'))
- up_grad: bfloat16 [8192, 16384], P('depth', ('row', 'col'))
- down_grad: bfloat16 [16384, 8192], P(('row', 'col'), 'depth')
The draws below stay inside these ranges and needn't reach their ends.
All inputs are finite; a program needn't handle non-finite values.
Results may differ from the reference program's by a relative error of at most 0.024.
Values may be sent and summed in bfloat16 or wider, within the bound.
No kernel may reach another device: no remote copies, remote signals or barrier semaphores. Data moves between devices by JAX's collectives and lax.ppermute only.
A program may use at most 128 MiB of HBM per device.

```python
import jax
import jax.numpy as jnp
from jax import lax

D = 8192
FF = 16384
TOK_BLK = 12
TOKENS = 768
N_DEPTH = 4
N_ROW = 16


def levels(stream_key, dims, shards, low, largest):
    def one(dim, parts):
        steps = jax.random.uniform(jax.random.fold_in(jax.random.fold_in(stream_key, 6), dim), (parts,), jnp.float32, low / len(shards), largest / len(shards))
        return jnp.repeat(jnp.exp(steps), dims[dim] // parts).reshape((-1,) + (1,) * (len(dims) - dim - 1))

    loudness = one(*shards[0])
    for cut in shards[1:]:
        loudness = loudness * one(*cut)
    return loudness


def noise(stream_key, extent, scale, bound, cuts=(), kind=jnp.bfloat16):
    values = scale * jax.random.normal(stream_key, extent, jnp.float32)
    if cuts:
        values = values * levels(stream_key, extent, cuts, -0.22, 0.18)
    return jnp.clip(values, -bound, bound).astype(kind)


def setup_inputs(seed: int = 0) -> dict:
    keys = jax.random.split(jax.random.key(seed), 6)
    tokens = noise(keys[0], (TOKENS, D), 1.0, 6.0, ((0, 64),))
    out_grad = noise(keys[1], (TOKENS, D), 0.1, 0.59765625, ((0, 64),))
    gate_weight = noise(keys[2], (D, FF), D ** -0.5, 0.0625, ((0, 4), (1, 64)))
    up_weight = noise(keys[3], (D, FF), D ** -0.5, 0.0625, ((0, 4), (1, 64)))
    down_weight = noise(keys[4], (FF, D), FF ** -0.5, 0.046875, ((0, 64), (1, 4)))
    return dict(tokens=tokens, out_grad=out_grad, gate_weight=gate_weight, up_weight=up_weight, down_weight=down_weight)


def contract_rows(left, right):
    return lax.dot_general(left, right, (((0,), (0,)), ((), ())), preferred_element_type=jnp.float32)


def contract_cols(left, right):
    return lax.dot_general(left, right, (((1,), (1,)), ((), ())), preferred_element_type=jnp.float32)


def reference(tokens, out_grad, gate_weight, up_weight, down_weight):
    gate = jnp.dot(tokens, gate_weight, preferred_element_type=jnp.float32)
    up = jnp.dot(tokens, up_weight, preferred_element_type=jnp.float32)
    sig = jax.nn.sigmoid(gate)
    act = gate * sig
    hidden = (act * up).astype(jnp.bfloat16)
    hidden_grad = contract_cols(out_grad, down_weight)
    gate_term = (hidden_grad * up * sig * (1.0 + gate * (1.0 - sig))).astype(jnp.bfloat16)
    up_term = (hidden_grad * act).astype(jnp.bfloat16)
    input_grad = contract_cols(gate_term, gate_weight) + contract_cols(up_term, up_weight)
    group = TOK_BLK * N_ROW
    gate_total = jnp.zeros(gate_weight.shape, jnp.float32)
    up_total = jnp.zeros(up_weight.shape, jnp.float32)
    down_total = jnp.zeros(down_weight.shape, jnp.float32)
    for k in range(N_DEPTH):
        lo = k * group
        tok_part = tokens[lo:lo + group]
        gate_total = gate_total + contract_rows(tok_part, gate_term[lo:lo + group]).astype(jnp.bfloat16).astype(jnp.float32)
        up_total = up_total + contract_rows(tok_part, up_term[lo:lo + group]).astype(jnp.bfloat16).astype(jnp.float32)
        down_total = down_total + contract_rows(hidden[lo:lo + group], out_grad[lo:lo + group]).astype(jnp.bfloat16).astype(jnp.float32)
    return (input_grad.astype(jnp.bfloat16), gate_total.astype(jnp.bfloat16),
            up_total.astype(jnp.bfloat16), down_total.astype(jnp.bfloat16))
```

```python
import jax
import jax.numpy as jnp
from jax import lax
from jax.sharding import Mesh
from jax.sharding import PartitionSpec as P

AXES = ("depth", "z", "yh", "yl", "core")
SIZES = (4, 8, 2, 2, 2)
BF16 = jnp.bfloat16
F32 = jnp.float32


def exchange(x, axes):
    return lax.all_to_all(x, axes, split_axis=0, concat_axis=0, tiled=True)


def gather(x, axes, n):
    return exchange(jnp.broadcast_to(x[None], (n,) + x.shape), axes)


def dot(left, right, dims):
    return lax.dot_general(left, right, (dims, ((), ())), preferred_element_type=F32)


def on_device(tokens, out_grad, gate_weight, up_weight, down_weight):
    yl = lax.axis_index("yl")
    core = lax.axis_index("core")
    part = core * 2 + yl

    def quarter(x):
        x = x.reshape(12, 4, 4, 512)
        x = lax.dynamic_index_in_dim(x, part, axis=2, keepdims=False)
        return x.transpose(1, 0, 2)

    with jax.named_scope("tokens_depth"):
        mine = jnp.stack([quarter(tokens), quarter(out_grad)], axis=1)
        mine = exchange(mine, "depth")
        mine = mine.transpose(1, 0, 2, 3).reshape(2, 48, 512)
    with jax.named_scope("tokens_z"):
        mine = gather(mine, "z", 8)
    with jax.named_scope("tokens_y"):
        mine = lax.all_gather(mine, ("yh", "yl"), axis=0, tiled=False)
    with jax.named_scope("tokens_core"):
        full = gather(mine, "core", 2)
        full = full.reshape(2, 2, 2, 8, 2, 48, 512)
        full = full.transpose(4, 1, 3, 5, 0, 2, 6).reshape(2, 768, 2048)
        tok, grad = full[0], full[1]

    with jax.named_scope("forward"):
        gate = dot(tok, gate_weight, ((1,), (0,)))
        up = dot(tok, up_weight, ((1,), (0,)))
        hidden_grad = dot(grad, down_weight, ((1,), (1,)))
        parts = jnp.concatenate([gate, up, hidden_grad], axis=1).astype(BF16)
    with jax.named_scope("sum_depth"):
        parts = exchange(parts.reshape(4, 192, 768), "depth")
        sums = jnp.sum(parts.astype(F32), axis=0)
    with jax.named_scope("terms"):
        gate, up, hidden_grad = sums[:, :256], sums[:, 256:512], sums[:, 512:]
        sig = jax.nn.sigmoid(gate)
        act = gate * sig
        hidden = (act * up).astype(BF16)
        gate_term = (hidden_grad * up * sig * (1.0 + gate * (1.0 - sig))).astype(BF16)
        up_term = (hidden_grad * act).astype(BF16)
        terms = jnp.concatenate([gate_term, up_term, hidden], axis=1)
    with jax.named_scope("terms_depth"):
        terms = gather(terms, "depth", 4).reshape(768, 768)
        gate_term, up_term, hidden = terms[:, :256], terms[:, 256:512], terms[:, 512:]

    with jax.named_scope("input_grad"):
        partial = dot(gate_term, gate_weight, ((1,), (1,))) + dot(up_term, up_weight, ((1,), (1,)))
        partial = partial.astype(BF16)
    with jax.named_scope("reduce_core"):
        x = partial.reshape(768, 2, 1024).transpose(1, 0, 2)
        x = jnp.sum(exchange(x, "core").astype(F32), axis=0).astype(BF16)
    with jax.named_scope("reduce_y"):
        x = x.reshape(2, 384, 2, 512).transpose(0, 2, 1, 3).reshape(4, 384, 512)
        x = jnp.sum(exchange(x, ("yh", "yl")).astype(F32), axis=0).astype(BF16)
    with jax.named_scope("reduce_z"):
        x = exchange(x.reshape(8, 48, 512), "z")
        x = jnp.sum(x.astype(F32), axis=0).astype(BF16)
    with jax.named_scope("place"):
        x = exchange(x.reshape(16, 3, 512), ("depth", "yl", "core"))
        x = x.reshape(4, 2, 2, 3, 512).transpose(3, 0, 2, 1, 4)
        input_grad = x.reshape(3, 8192)

    with jax.named_scope("weight_grads"):
        gate_grad = dot(tok, gate_term, ((0,), (0,))).astype(BF16)
        up_grad = dot(tok, up_term, ((0,), (0,))).astype(BF16)
        down_grad = dot(hidden, grad, ((0,), (0,))).astype(BF16)
    return input_grad, gate_grad, up_grad, down_grad


def solution(mesh):
    fine = Mesh(mesh.devices.reshape(SIZES), AXES)
    row, col = ("z", "yh"), ("yl", "core")
    return jax.shard_map(
        on_device,
        mesh=fine,
        in_specs=(
            P(("depth",) + row, None),
            P(("depth",) + row, None),
            P("depth", row + col),
            P("depth", row + col),
            P(row + col, "depth"),
        ),
        out_specs=(
            P(("depth",) + row + col, None),
            P("depth", row + col),
            P("depth", row + col),
            P(row + col, "depth"),
        ),
        check_vma=False,
    )
```

```python
import jax
import jax.numpy as jnp
from jax import lax
from jax.experimental import pallas as pl
from jax.experimental.pallas import tpu as pltpu
from jax.sharding import Mesh
from jax.sharding import PartitionSpec as P

AXES = ("depth", "z", "yh", "yl", "core")
SIZES = (4, 8, 2, 2, 2)
BF16 = jnp.bfloat16
F32 = jnp.float32
HALF = 384
QUART = 192
PART = 512
FF = 256


def exchange(x, axes):
    return lax.all_to_all(x, axes, split_axis=0, concat_axis=0, tiled=True)


def swap_core(x):
    return lax.ppermute(x, "core", [(0, 1), (1, 0)])


def swap_near(x):
    return lax.ppermute(x, "yl", [(0, 1), (1, 0)])


def swap_far(x):
    return lax.ppermute(x, ("yh", "yl"), [(0, 3), (3, 0), (1, 2), (2, 1)])


def swap_opposite(x):
    return lax.ppermute(x, "yh", [(0, 1), (1, 0)])


def dot(left, right, dims):
    return lax.dot_general(left, right, (dims, ((), ())), preferred_element_type=F32)


def call(body, outs, args, flops, scalars=0):
    size = sum(a.size * a.dtype.itemsize for a in args)
    size += sum(o.size * o.dtype.itemsize for o in outs)
    specs = [pl.BlockSpec(memory_space=pltpu.SMEM)] * scalars
    specs += [pl.BlockSpec(memory_space=pltpu.VMEM)] * (len(args) - scalars)
    return pl.pallas_call(
        body,
        out_shape=outs,
        in_specs=specs,
        out_specs=[pl.BlockSpec(memory_space=pltpu.VMEM)] * len(outs),
        compiler_params=pltpu.CompilerParams(vmem_limit_bytes=40 << 20),
        cost_estimate=pl.CostEstimate(flops=flops, bytes_accessed=size, transcendentals=0),
    )(*args)


def out(shape, dtype):
    return jax.ShapeDtypeStruct(shape, dtype)


def part(k):
    return pl.ds(pl.multiple_of(k * PART, PART), PART)


def blocks(refs):
    own, near, far, opp_a, opp_b = refs[:5]
    own_s, near_s, far_s, opp_as, opp_bs = refs[5:]
    yield 0, HALF, (own, near, own_s, near_s)
    yield HALF, QUART, (opp_a, far.at[:QUART], opp_as, far_s.at[:QUART])
    yield HALF + QUART, QUART, (opp_b, far.at[QUART:], opp_bs, far_s.at[QUART:])


def forward_tok(idx, gate_w, up_w, *refs):
    o = refs[-1]
    for lo, rows, xs in blocks(refs[:-1]):
        for w, c in ((gate_w, 0), (up_w, FF)):
            total = sum(dot(x[...], w[part(idx[k]), :], ((1,), (0,))) for k, x in enumerate(xs))
            o[lo:lo + rows, c:c + FF] = total.astype(BF16)


def forward_grad(idx, down_w, *refs):
    o = refs[-1]
    for lo, rows, xs in blocks(refs[:-1]):
        total = sum(dot(x[...], down_w[:, part(idx[k])], ((1,), (1,))) for k, x in enumerate(xs))
        o[lo:lo + rows, :] = total.astype(BF16)


def total_of(ref):
    total = ref[0].astype(F32)
    for i in range(1, ref.shape[0]):
        total = total + ref[i].astype(F32)
    return total


def act_terms(parts, hidden_o, act_o, slope_o):
    total = total_of(parts)
    gate, up = total[:, :FF], total[:, FF:]
    sig = 1.0 / (1.0 + jnp.exp(-gate))
    act = gate * sig
    hidden = (act * up).astype(BF16)
    for i in range(4):
        hidden_o[i] = hidden
    act_o[...] = act
    slope_o[...] = up * sig * (1.0 + gate * (1.0 - sig))


def grad_terms(parts, act, slope, o):
    hidden_grad = total_of(parts)
    gate_term = (hidden_grad * slope[...]).astype(BF16)
    up_term = (hidden_grad * act[...]).astype(BF16)
    for i in range(4):
        o[i, :, :FF] = gate_term
        o[i, :, FF:] = up_term


def backward_other(idx, terms, gate_w, up_w, o):
    for c, k in ((0, 2), (PART, 3)):
        for lo in (0, HALF):
            rows = slice(lo, lo + HALF)
            total = dot(terms[rows, :FF], gate_w[part(idx[k]), :], ((1,), (1,)))
            total += dot(terms[rows, FF:], up_w[part(idx[k]), :], ((1,), (1,)))
            o[rows, c:c + PART] = total.astype(BF16)


def backward_own(idx, terms, gate_w, up_w, came, keep, near, far, opposite):
    for c, k in ((0, 0), (PART, 1)):
        for lo in (0, HALF):
            rows = slice(lo, lo + HALF)
            total = dot(terms[rows, :FF], gate_w[part(idx[k]), :], ((1,), (1,)))
            total += dot(terms[rows, FF:], up_w[part(idx[k]), :], ((1,), (1,)))
            total += came[rows, c:c + PART].astype(F32)
            o = {(0, 0): keep, (1, 0): near, (1, HALF): far, (0, HALF): opposite}[(k, lo)]
            o[...] = total.astype(o.dtype)


def sum_y(keep, near, far, opposite, o):
    total = keep[...] + near[...].astype(F32) + far[...].astype(F32) + opposite[...].astype(F32)
    o[...] = total.astype(BF16)


def sum_z(parts, o):
    o[...] = total_of(parts).astype(BF16)


def gate_up_grads(idx, terms, *refs):
    gate_o, up_o = refs[-2:]
    bl = list(blocks(refs[:-2]))
    for k in range(4):
        total = sum(dot(xs[k][...], terms[lo:lo + rows, :], ((0,), (0,))) for lo, rows, xs in bl)
        gate_o[part(idx[k]), :] = total[:, :FF].astype(BF16)
        up_o[part(idx[k]), :] = total[:, FF:].astype(BF16)


def down_grads(idx, hidden, *refs):
    o = refs[-1]
    bl = list(blocks(refs[:-1]))
    for k in range(4):
        total = sum(dot(hidden[lo:lo + rows, :], xs[k][...], ((0,), (0,))) for lo, rows, xs in bl)
        o[:, part(idx[k])] = total.astype(BF16)


def collect(x, mine):
    x = x.reshape(12, 4, 4, PART)
    x = lax.dynamic_index_in_dim(x, mine, axis=2, keepdims=False)
    x = x.transpose(1, 0, 2)
    x = jnp.broadcast_to(x[None], (8, 4, 12, PART)).reshape(32, 12, PART)
    own = exchange(x, ("z", "depth")).reshape(HALF, PART)
    near, far = swap_near(own), swap_far(own)
    opp_a = swap_near(far[:QUART])
    opp_b = swap_far(near[QUART:])
    direct = [own, near, far, opp_a, opp_b]
    return direct + [swap_core(b) for b in direct]


def on_device(tokens, out_grad, gate_weight, up_weight, down_weight):
    yl = lax.axis_index("yl")
    core = lax.axis_index("core")
    mine = core * 2 + yl
    idx = jnp.bitwise_xor(mine, jnp.arange(4, dtype=jnp.int32))

    with jax.named_scope("collect_tokens"):
        tok = collect(tokens, mine)
    with jax.named_scope("collect_grads"):
        grad = collect(out_grad, mine)
    flops = 2 * 768 * 2048 * FF
    with jax.named_scope("forward_tok"):
        (parts,) = call(forward_tok, [out((768, 512), BF16)], [idx, gate_weight, up_weight] + tok, 2 * flops, 1)
    with jax.named_scope("sum_gate_up"):
        parts = exchange(parts.reshape(4, QUART, 512), "depth")
        hidden, act, slope = call(
            act_terms,
            [out((4, QUART, FF), BF16), out((QUART, FF), F32), out((QUART, FF), F32)],
            [parts], 10 * QUART * FF)
    with jax.named_scope("forward_grad"):
        (parts,) = call(forward_grad, [out((768, FF), BF16)], [idx, down_weight] + grad, flops, 1)
    with jax.named_scope("sum_hidden_grad"):
        parts = exchange(parts.reshape(4, QUART, FF), "depth")
        (terms,) = call(grad_terms, [out((4, QUART, 512), BF16)], [parts, act, slope], 10 * QUART * FF)
    with jax.named_scope("gather_terms"):
        terms = exchange(terms, "depth").reshape(768, 512)
    with jax.named_scope("gather_hidden"):
        hidden = exchange(hidden, "depth").reshape(768, FF)

    with jax.named_scope("backward_other"):
        (send,) = call(backward_other, [out((768, 1024), BF16)], [idx, terms, gate_weight, up_weight], flops, 1)
        came = swap_core(send)
    with jax.named_scope("backward_own"):
        piece = out((HALF, PART), BF16)
        keep, near, far, opposite = call(
            backward_own, [out((HALF, PART), F32), piece, piece, piece],
            [idx, terms, gate_weight, up_weight, came], flops, 1)
    with jax.named_scope("reduce_y"):
        opposite, near, far = swap_opposite(opposite), swap_near(near), swap_far(far)
        (x,) = call(sum_y, [piece], [keep, near, far, opposite], 3 * HALF * PART)
    with jax.named_scope("reduce_z"):
        x = exchange(x.reshape(8, 48, PART), "z")
        (x,) = call(sum_z, [out((48, PART), BF16)], [x], 8 * 48 * PART)
    with jax.named_scope("place"):
        x = exchange(x.reshape(16, 3, PART), ("depth", "yl", "core"))
        x = x.reshape(4, 2, 2, 3, PART).transpose(3, 0, 2, 1, 4)
        input_grad = x.reshape(3, 8192)

    with jax.named_scope("gate_up_grads"):
        weight = out((2048, FF), BF16)
        gate_grad, up_grad = call(gate_up_grads, [weight, weight], [idx, terms] + tok, 2 * flops, 1)
    with jax.named_scope("down_grads"):
        (down_grad,) = call(down_grads, [out((FF, 2048), BF16)], [idx, hidden] + grad, flops, 1)
    return input_grad, gate_grad, up_grad, down_grad


def solution(mesh):
    fine = Mesh(mesh.devices.reshape(SIZES), AXES)
    row, col = ("z", "yh"), ("yl", "core")
    return jax.shard_map(
        on_device,
        mesh=fine,
        in_specs=(
            P(("depth",) + row, None),
            P(("depth",) + row, None),
            P("depth", row + col),
            P("depth", row + col),
            P(row + col, "depth"),
        ),
        out_specs=(
            P(("depth",) + row + col, None),
            P("depth", row + col),
            P("depth", row + col),
            P(row + col, "depth"),
        ),
        check_vma=False,
    )
```

```python
import jax
import jax.numpy as jnp
from jax import lax
from jax.experimental import pallas as pl
from jax.experimental.pallas import tpu as pltpu
from jax.sharding import Mesh
from jax.sharding import PartitionSpec as P

AXES = ("depth", "z", "yh", "yl", "core")
SIZES = (4, 8, 2, 2, 2)
BF16 = jnp.bfloat16
F32 = jnp.float32
HALF = 384
QUART = 192
GROUP = 96
WIDE = 2048
PART = 512
FF = 256


def exchange(x, axes):
    return lax.all_to_all(x, axes, split_axis=0, concat_axis=0, tiled=True)


def swap_core(x):
    return lax.ppermute(x, "core", [(0, 1), (1, 0)])


def swap_near(x):
    return lax.ppermute(x, "yl", [(0, 1), (1, 0)])


def swap_far(x):
    return lax.ppermute(x, ("yh", "yl"), [(0, 3), (3, 0), (1, 2), (2, 1)])


def swap_opposite(x):
    return lax.ppermute(x, "yh", [(0, 1), (1, 0)])


def swap_depth(x, k):
    return lax.ppermute(x, "depth", [(i, i ^ k) for i in range(4)])


def dot(left, right, dims):
    return lax.dot_general(left, right, (dims, ((), ())), preferred_element_type=F32)


def call(body, outs, args, flops, scratch=()):
    size = sum(a.size * a.dtype.itemsize for a in args)
    size += sum(o.size * o.dtype.itemsize for o in outs)
    vmem = pl.BlockSpec(memory_space=pltpu.VMEM)
    return pl.pallas_call(
        body,
        out_shape=outs,
        in_specs=[vmem] * len(args),
        out_specs=[vmem] * len(outs),
        scratch_shapes=list(scratch),
        compiler_params=pltpu.CompilerParams(vmem_limit_bytes=20 << 20),
        cost_estimate=pl.CostEstimate(flops=flops, bytes_accessed=size, transcendentals=0),
    )(*args)


def out(shape, dtype):
    return jax.ShapeDtypeStruct(shape, dtype)


def rows_of(k, size):
    return pl.ds(pl.multiple_of(k * size, size), size)


def column_parts():
    mine = lax.axis_index("core") * 2 + lax.axis_index("yl")
    return [rows_of(mine ^ k, PART) for k in range(4)]


def pack(tokens, out_grad, o, scr):
    mine = lax.axis_index("core") * 2 + lax.axis_index("yl")
    for kind, x in enumerate((tokens, out_grad)):
        for d in range(4):
            for c in range(4):
                lane = pl.multiple_of(mine * PART + d * WIDE + c * 128, 128)
                scr[pl.ds(c, 12, stride=4), :] = x[:, pl.ds(lane, 128)].astype(F32)
            block = scr[...].astype(BF16)
            for z in range(8):
                o[z * 4 + d, kind] = block


def unpack(came, tok_o, grad_o, scr):
    for kind, o in enumerate((tok_o, grad_o)):
        for i in range(32):
            scr[i * 48:(i + 1) * 48, :] = came[i, kind].astype(F32)
        for t in range(12):
            for c in range(4):
                block = scr[pl.ds(t * 4 + c, 32, stride=48), :]
                o[t * 32:(t + 1) * 32, c * 128:(c + 1) * 128] = block.astype(BF16)


def blocks(refs):
    own, near, far, opp_a, opp_b, own_s, near_s, far_s, opp_as, opp_bs = refs
    every, lo, hi = slice(0, HALF), slice(0, QUART), slice(QUART, HALF)
    yield 0, HALF, ((own, every), (near, every), (own_s, every), (near_s, every))
    yield HALF, QUART, ((opp_a, lo), (far, lo), (opp_as, lo), (far_s, lo))
    yield HALF + QUART, QUART, ((opp_b, lo), (far, hi), (opp_bs, lo), (far_s, hi))


def spread_depth(scr, outs):
    d = lax.axis_index("depth")
    for k, o in enumerate(outs):
        o[...] = scr[rows_of(d ^ k, QUART), :].astype(o.dtype)


def forward_tok(gate_w, up_w, *refs):
    outs, scr = refs[10:14], refs[14]
    ps = column_parts()
    for lo, rows, xs in blocks(refs[:10]):
        for w, c in ((gate_w, 0), (up_w, FF)):
            total = sum(dot(x[r, :], w[p, :], ((1,), (0,))) for p, (x, r) in zip(ps, xs))
            scr[lo:lo + rows, c:c + FF] = total
    spread_depth(scr, outs)


def forward_grad(down_w, *refs):
    outs, scr = refs[10:14], refs[14]
    ps = column_parts()
    for lo, rows, xs in blocks(refs[:10]):
        total = sum(dot(x[r, :], down_w[:, p], ((1,), (1,))) for p, (x, r) in zip(ps, xs))
        scr[lo:lo + rows, :] = total
    spread_depth(scr, outs)


def grad_terms(*refs):
    total, hidden_grad = (sum(r[...].astype(F32) for r in refs[i:i + 4]) for i in (0, 4))
    terms_o, hidden_o = refs[8:]
    gate, up = total[:, :FF], total[:, FF:]
    sig = 1.0 / (1.0 + jnp.exp(-gate))
    act = gate * sig
    hidden_o[...] = (act * up).astype(BF16)
    terms_o[:, :FF] = (hidden_grad * up * sig * (1.0 + gate * (1.0 - sig))).astype(BF16)
    terms_o[:, FF:] = (hidden_grad * act).astype(BF16)


def gather_rows(refs, scr):
    d = lax.axis_index("depth")
    for k, r in enumerate(refs):
        scr[rows_of(d ^ k, QUART), :] = r[...]


def input_rows(terms, core, pick):
    yl = lax.axis_index("yl")
    for ab in range(2):
        for j in range(2):
            i = ab * 2 + j
            pick[i * GROUP:(i + 1) * GROUP, :] = terms[rows_of(ab * 4 + (yl ^ j) * 2 + core, GROUP), :]


def backward_other(t0, t1, t2, t3, gate_w, up_w, terms, o, pick):
    gather_rows((t0, t1, t2, t3), terms)
    input_rows(terms, 1 - lax.axis_index("core"), pick)
    for p in range(4):
        cols = slice(p * PART, (p + 1) * PART)
        total = dot(pick[:, :FF], gate_w[cols, :], ((1,), (1,)))
        total += dot(pick[:, FF:], up_w[cols, :], ((1,), (1,)))
        o[:, cols] = total.astype(BF16)


def backward_own(terms, gate_w, up_w, came, keep, near, opposite, far, pick):
    input_rows(terms, lax.axis_index("core"), pick)
    for p in range(4):
        cols = slice(p * PART, (p + 1) * PART)
        total = dot(pick[:, :FF], gate_w[cols, :], ((1,), (1,)))
        total += dot(pick[:, FF:], up_w[cols, :], ((1,), (1,)))
        total += came[:, cols].astype(F32)
        for i, o in enumerate((keep, near, opposite, far)):
            o[:, cols] = total[i * GROUP:(i + 1) * GROUP, :].astype(o.dtype)


def sum_y(keep, near, far, opposite, o, scr):
    for r in range(3):
        for c in range(16):
            at = (slice(r * 32, (r + 1) * 32), slice(c * 128, (c + 1) * 128))
            total = keep[at] + near[at].astype(F32) + far[at].astype(F32) + opposite[at].astype(F32)
            scr[pl.ds(r * 16 + c, 32, stride=48), :] = total
    for i in range(32):
        o[i] = scr[i * 48:(i + 1) * 48, :].astype(BF16)


def sum_z(came, o, scr):
    for d in range(4):
        total = came[d].astype(F32)
        for z in range(1, 8):
            total = total + came[z * 4 + d].astype(F32)
        scr[...] = total
        for c in range(16):
            o[:, d * WIDE + c * 128:d * WIDE + (c + 1) * 128] = scr[pl.ds(c, 3, stride=16), :].astype(BF16)


def gate_up_grads(terms, *refs):
    gate_o, up_o = refs[10:]
    bl = list(blocks(refs[:10]))
    for k, p in enumerate(column_parts()):
        total = sum(dot(xs[k][0][xs[k][1], :], terms[lo:lo + rows, :], ((0,), (0,))) for lo, rows, xs in bl)
        gate_o[p, :] = total[:, :FF].astype(BF16)
        up_o[p, :] = total[:, FF:].astype(BF16)


def down_grads(h0, h1, h2, h3, *refs):
    o, hidden = refs[10:]
    gather_rows((h0, h1, h2, h3), hidden)
    bl = list(blocks(refs[:10]))
    for k, p in enumerate(column_parts()):
        total = sum(dot(hidden[lo:lo + rows, :], xs[k][0][xs[k][1], :], ((0,), (0,))) for lo, rows, xs in bl)
        o[:, p] = total.astype(BF16)


def collect(own, near, far):
    opp_a = swap_near(far[:QUART])
    opp_b = swap_far(near[QUART:])
    direct = [own, near, far, opp_a, opp_b]
    return direct + [swap_core(b) for b in direct]


def on_device(tokens, out_grad, gate_weight, up_weight, down_weight):
    block = out((HALF, PART), BF16)
    with jax.named_scope("slice_out"):
        (x,) = call(pack, [out((32, 2, 48, 128), BF16)], [tokens, out_grad], 0, [pltpu.VMEM((48, 128), F32)])
        x = exchange(x, ("z", "depth"))
        tok, grad = call(unpack, [block, block], [x], 0, [pltpu.VMEM((1536, 128), F32)])
    with jax.named_scope("collect_tokens"):
        near, far = swap_near(tok), swap_far(tok)
        near, far, grad = lax.optimization_barrier((near, far, grad))
        tok = collect(tok, near, far)
    with jax.named_scope("collect_grads"):
        grad = collect(grad, swap_near(grad), swap_far(grad))

    flops = 2 * 768 * 2048 * FF
    with jax.named_scope("forward_tok"):
        part = out((QUART, 2 * FF), BF16)
        own, *others = call(
            forward_tok, [out((QUART, 2 * FF), F32), part, part, part],
            [gate_weight, up_weight] + tok, 2 * flops, [pltpu.VMEM((768, 2 * FF), F32)])
    with jax.named_scope("sum_gate_up"):
        gate_up = [own] + [swap_depth(x, k + 1) for k, x in enumerate(others)]
    with jax.named_scope("forward_grad"):
        part = out((QUART, FF), BF16)
        own, *others = call(
            forward_grad, [out((QUART, FF), F32), part, part, part],
            [down_weight] + grad, flops, [pltpu.VMEM((768, FF), F32)])
    with jax.named_scope("sum_hidden_grad"):
        hidden_grad = [own] + [swap_depth(x, k + 1) for k, x in enumerate(others)]
    with jax.named_scope("terms"):
        terms, hidden = call(
            grad_terms, [out((QUART, 2 * FF), BF16), out((QUART, FF), BF16)], gate_up + hidden_grad, 20 * QUART * FF)
    with jax.named_scope("gather_terms"):
        terms = [terms] + [swap_depth(terms, k) for k in (1, 2, 3)]

    with jax.named_scope("backward_other"):
        terms, send = call(
            backward_other, [out((768, 2 * FF), BF16), out((HALF, WIDE), BF16)],
            terms + [gate_weight, up_weight], flops, [pltpu.VMEM((HALF, 2 * FF), BF16)])
        send, hidden = lax.optimization_barrier((send, hidden))
        came = swap_core(send)
    with jax.named_scope("gather_hidden"):
        hidden = [hidden] + [swap_depth(hidden, k) for k in (1, 2, 3)]
    with jax.named_scope("backward_own"):
        piece = out((GROUP, WIDE), BF16)
        keep, near, opposite, far = call(
            backward_own, [out((GROUP, WIDE), F32), piece, piece, piece],
            [terms, gate_weight, up_weight, came], flops, [pltpu.VMEM((HALF, 2 * FF), BF16)])
    with jax.named_scope("reduce_y"):
        opposite, near, far = swap_opposite(opposite), swap_near(near), swap_far(far)
    with jax.named_scope("gate_up_grads"):
        weight = out((2048, FF), BF16)
        gate_grad, up_grad = call(gate_up_grads, [weight, weight], [terms] + tok, 2 * flops)
    with jax.named_scope("down_grads"):
        (down_grad,) = call(
            down_grads, [out((FF, 2048), BF16)], hidden + grad, flops, [pltpu.VMEM((768, FF), BF16)])
    with jax.named_scope("reduce_z"):
        (x,) = call(
            sum_y, [out((32, 48, 128), BF16)], [keep, near, far, opposite], 3 * GROUP * WIDE,
            [pltpu.VMEM((1536, 128), F32)])
        x, gate_grad, up_grad, down_grad = lax.optimization_barrier((x, gate_grad, up_grad, down_grad))
        x = exchange(x, ("z", "depth"))
        (input_grad,) = call(sum_z, [out((3, 8192), BF16)], [x], 0, [pltpu.VMEM((48, 128), F32)])
    return input_grad, gate_grad, up_grad, down_grad


def solution(mesh):
    fine = Mesh(mesh.devices.reshape(SIZES), AXES)
    row, col = ("z", "yh"), ("yl", "core")
    return jax.shard_map(
        on_device,
        mesh=fine,
        in_specs=(
            P(("depth",) + row, None),
            P(("depth",) + row, None),
            P("depth", row + col),
            P("depth", row + col),
            P(row + col, "depth"),
        ),
        out_specs=(
            P(("depth",) + row + col, None),
            P("depth", row + col),
            P("depth", row + col),
            P(row + col, "depth"),
        ),
        check_vma=False,
    )
```

```python
import jax
import jax.numpy as jnp
from jax import lax
from jax.experimental import pallas as pl
from jax.experimental.pallas import tpu as pltpu
from jax.sharding import Mesh
from jax.sharding import PartitionSpec as P

AXES = ("depth", "z", "yh", "yl", "core")
SIZES = (4, 8, 2, 2, 2)
BF16 = jnp.bfloat16
F32 = jnp.float32
HALF = 384
QUART = 192
GROUP = 96
WIDE = 2048
PART = 512
FF = 256


def exchange(x, axes):
    return lax.all_to_all(x, axes, split_axis=0, concat_axis=0, tiled=True)


def swap_core(x):
    return lax.ppermute(x, "core", [(0, 1), (1, 0)])


def swap_near(x):
    return lax.ppermute(x, "yl", [(0, 1), (1, 0)])


def swap_far(x):
    return lax.ppermute(x, ("yh", "yl"), [(0, 3), (3, 0), (1, 2), (2, 1)])


def swap_opposite(x):
    return lax.ppermute(x, "yh", [(0, 1), (1, 0)])


def swap_depth(x, k):
    return lax.ppermute(x, "depth", [(i, i ^ k) for i in range(4)])


def dot(left, right, dims):
    return lax.dot_general(left, right, (dims, ((), ())), preferred_element_type=F32)


def call(body, outs, args, flops, scratch=()):
    size = sum(a.size * a.dtype.itemsize for a in args)
    size += sum(o.size * o.dtype.itemsize for o in outs)
    vmem = pl.BlockSpec(memory_space=pltpu.VMEM)
    return list(pl.pallas_call(
        body,
        out_shape=outs,
        in_specs=[vmem] * len(args),
        out_specs=[vmem] * len(outs),
        scratch_shapes=list(scratch),
        compiler_params=pltpu.CompilerParams(vmem_limit_bytes=20 << 20),
        cost_estimate=pl.CostEstimate(flops=flops, bytes_accessed=size, transcendentals=0),
    )(*args))


def out(shape, dtype):
    return jax.ShapeDtypeStruct(shape, dtype)


def rows_of(k, size):
    return pl.ds(pl.multiple_of(k * size, size), size)


def column_parts():
    mine = lax.axis_index("core") * 2 + lax.axis_index("yl")
    return [rows_of(mine ^ k, PART) for k in range(4)]


def pack(tokens, out_grad, o, scr):
    mine = lax.axis_index("core") * 2 + lax.axis_index("yl")
    for kind, x in enumerate((tokens, out_grad)):
        for d in range(4):
            for c in range(4):
                lane = pl.multiple_of(mine * PART + d * WIDE + c * 128, 128)
                scr[pl.ds(c, 12, stride=4), :] = x[:, pl.ds(lane, 128)].astype(F32)
            block = scr[...].astype(BF16)
            for z in range(8):
                o[z * 4 + d, kind] = block


def unpack(came, lo_o, hi_o, scr):
    for kind in range(2):
        for i in range(32):
            scr[i * 48:(i + 1) * 48, :] = came[i, kind].astype(F32)
        for half, o in enumerate((lo_o, hi_o)):
            for t in range(6):
                for c in range(4):
                    block = scr[pl.ds((half * 6 + t) * 4 + c, 32, stride=48), :]
                    o[kind, t * 32:(t + 1) * 32, c * 128:(c + 1) * 128] = block.astype(BF16)


def forward(gate_w, up_w, down_w, *refs):
    xs, outs, scr = refs[:8], refs[8:12], refs[12]
    ps = column_parts()
    for half in range(2):
        rows = slice(half * QUART, (half + 1) * QUART)
        some = xs[half::2]
        for w, c in ((gate_w, 0), (up_w, FF)):
            scr[rows, c:c + FF] = sum(dot(x[0], w[p, :], ((1,), (0,))) for p, x in zip(ps, some))
        scr[rows, 2 * FF:] = sum(dot(x[1], down_w[:, p], ((1,), (1,))) for p, x in zip(ps, some))
    d = lax.axis_index("depth")
    for k, o in enumerate(outs):
        o[...] = scr[rows_of(d ^ k, GROUP), :].astype(o.dtype)


def grad_terms(p0, p1, p2, p3, *refs):
    terms_o, hidden_o = refs[-2:]
    total = sum(r[...].astype(F32) for r in (p0, p1, p2, p3))
    gate, up, hidden_grad = total[:, :FF], total[:, FF:2 * FF], total[:, 2 * FF:]
    sig = 1.0 / (1.0 + jnp.exp(-gate))
    act = gate * sig
    hidden = (act * up).astype(BF16)
    if len(refs) == 3:
        hidden_o[0] = refs[0][...]
        hidden_o[1] = hidden
    else:
        hidden_o[...] = hidden
    terms_o[:, :FF] = (hidden_grad * up * sig * (1.0 + gate * (1.0 - sig))).astype(BF16)
    terms_o[:, FF:] = (hidden_grad * act).astype(BF16)


def input_rows(terms, core, pick):
    yl = lax.axis_index("yl")
    for j in range(2):
        pick[j * GROUP:(j + 1) * GROUP, :] = terms[rows_of((yl ^ j) * 2 + core, GROUP), :]


def backward_other(t0, t1, t2, t3, gate_w, up_w, terms, o, pick):
    d = lax.axis_index("depth")
    for k, t in enumerate((t0, t1, t2, t3)):
        terms[rows_of(d ^ k, GROUP), :] = t[...]
    input_rows(terms, 1 - lax.axis_index("core"), pick)
    for p in range(4):
        cols = slice(p * PART, (p + 1) * PART)
        total = dot(pick[:, :FF], gate_w[cols, :], ((1,), (1,)))
        total += dot(pick[:, FF:], up_w[cols, :], ((1,), (1,)))
        o[:, cols] = total.astype(BF16)


def backward_own(terms, gate_w, up_w, came, here, away, pick):
    input_rows(terms, lax.axis_index("core"), pick)
    for p in range(4):
        cols = slice(p * PART, (p + 1) * PART)
        total = dot(pick[:, :FF], gate_w[cols, :], ((1,), (1,)))
        total += dot(pick[:, FF:], up_w[cols, :], ((1,), (1,)))
        total += came[:, cols].astype(F32)
        here[:, cols] = total[:GROUP].astype(here.dtype)
        away[:, cols] = total[GROUP:].astype(away.dtype)


def sum_y(keep, near, far, opposite, o, scr):
    for r in range(3):
        for c in range(16):
            at = (slice(r * 32, (r + 1) * 32), slice(c * 128, (c + 1) * 128))
            total = keep[at] + near[at].astype(F32) + far[at].astype(F32) + opposite[at].astype(F32)
            scr[pl.ds(r * 16 + c, 32, stride=48), :] = total
    for i in range(32):
        o[i] = scr[i * 48:(i + 1) * 48, :].astype(BF16)


def sum_z(came, o, scr):
    for d in range(4):
        total = came[d].astype(F32)
        for z in range(1, 8):
            total = total + came[z * 4 + d].astype(F32)
        scr[...] = total
        for c in range(16):
            o[:, d * WIDE + c * 128:d * WIDE + (c + 1) * 128] = scr[pl.ds(c, 3, stride=16), :].astype(BF16)


def halves(refs):
    for i in range(4):
        yield i * QUART, refs[i // 2 * 8 + i % 2:i // 2 * 8 + 8:2]


def gate_up_grads(terms_a, terms_b, *refs):
    gate_o, up_o = refs[16:]
    for k, p in enumerate(column_parts()):
        total = 0.0
        for lo, xs in halves(refs):
            t = (terms_a, terms_b)[lo // HALF]
            total += dot(xs[k][0], t[lo % HALF:lo % HALF + QUART, :], ((0,), (0,)))
        gate_o[p, :] = total[:, :FF].astype(BF16)
        up_o[p, :] = total[:, FF:].astype(BF16)


def down_grads(h0, h1, h2, h3, *refs):
    o, hidden = refs[16:]
    d = lax.axis_index("depth")
    for k, h in enumerate((h0, h1, h2, h3)):
        for chunk in range(2):
            hidden[rows_of(chunk * 4 + (d ^ k), GROUP), :] = h[chunk]
    for k, p in enumerate(column_parts()):
        total = sum(dot(hidden[lo:lo + QUART, :], xs[k][1], ((0,), (0,))) for lo, xs in halves(refs))
        o[:, p] = total.astype(BF16)


def on_device(tokens, out_grad, gate_weight, up_weight, down_weight):
    block = out((2, QUART, PART), BF16)
    weights = [gate_weight, up_weight, down_weight]
    flops = HALF * 2048 * FF
    with jax.named_scope("slice_out"):
        (x,) = call(pack, [out((32, 2, 48, 128), BF16)], [tokens, out_grad], 0, [pltpu.VMEM((48, 128), F32)])
        x = exchange(x, ("z", "depth"))
        own = call(unpack, [block, block], [x], 0, [pltpu.VMEM((1536, 128), F32)])

    def forward_chunk(blocks):
        part = out((GROUP, 3 * FF), BF16)
        return call(
            forward, [out((GROUP, 3 * FF), F32), part, part, part], weights + blocks, 6 * flops,
            [pltpu.VMEM((HALF, 3 * FF), F32)])

    def sum_depth(parts):
        return [parts[0]] + [swap_depth(parts[k], k) for k in (1, 2, 3)]

    def backward_in(terms):
        return call(
            backward_other, [out((HALF, 2 * FF), BF16), out((QUART, WIDE), BF16)],
            [terms] + [swap_depth(terms, k) for k in (1, 2, 3)] + weights[:2], 2 * flops,
            [pltpu.VMEM((QUART, 2 * FF), BF16)])

    def backward_out(terms, came, dtype):
        return call(
            backward_own, [out((GROUP, WIDE), dtype), out((GROUP, WIDE), BF16)],
            [terms] + weights[:2] + [came], 2 * flops, [pltpu.VMEM((QUART, 2 * FF), BF16)])

    with jax.named_scope("collect"):
        near = [swap_near(x) for x in own]
        far = [swap_far(x) for x in own]
        opposite = [swap_near(far[0]), swap_far(near[1])]
        block_a = own + near + [swap_core(x) for x in own + near]
    with jax.named_scope("forward_a"):
        parts_a = forward_chunk(block_a)
        opposite = list(lax.optimization_barrier((*opposite, parts_a[1]))[:2])
        parts_a = sum_depth(parts_a)
    with jax.named_scope("collect_b"):
        block_b = opposite + far + [swap_core(x) for x in opposite + far]
    with jax.named_scope("forward_b"):
        parts_b = sum_depth(forward_chunk(block_b))
    with jax.named_scope("terms_a"):
        piece = [out((GROUP, 2 * FF), BF16), out((GROUP, FF), BF16)]
        terms_a, hidden = call(grad_terms, piece, parts_a, 20 * GROUP * FF)
    with jax.named_scope("terms_b"):
        piece = [out((GROUP, 2 * FF), BF16), out((2, GROUP, FF), BF16)]
        terms_b, hidden = call(grad_terms, piece, parts_b + [hidden], 20 * GROUP * FF)
    with jax.named_scope("backward_a"):
        terms_a, send = backward_in(terms_a)
        keep, near = backward_out(terms_a, swap_core(send), F32)
        near = swap_near(near)
    with jax.named_scope("backward_b"):
        terms_b, send = backward_in(terms_b)
        send, hidden = lax.optimization_barrier((send, hidden))
        opposite, far = backward_out(terms_b, swap_core(send), BF16)
        opposite, far = swap_opposite(opposite), swap_far(far)
    with jax.named_scope("gather_hidden"):
        hidden = [hidden] + [swap_depth(hidden, k) for k in (1, 2, 3)]
    with jax.named_scope("gate_up_grads"):
        weight = out((2048, FF), BF16)
        gate_grad, up_grad = call(
            gate_up_grads, [weight, weight], [terms_a, terms_b] + block_a + block_b, 8 * flops)
    with jax.named_scope("down_grads"):
        (down_grad,) = call(
            down_grads, [out((FF, 2048), BF16)], hidden + block_a + block_b, 4 * flops,
            [pltpu.VMEM((768, FF), BF16)])
    with jax.named_scope("reduce_z"):
        (x,) = call(
            sum_y, [out((32, 48, 128), BF16)], [keep, near, far, opposite], 3 * GROUP * WIDE,
            [pltpu.VMEM((1536, 128), F32)])
        x, gate_grad, up_grad, down_grad = lax.optimization_barrier((x, gate_grad, up_grad, down_grad))
        x = exchange(x, ("z", "depth"))
        (input_grad,) = call(sum_z, [out((3, 8192), BF16)], [x], 0, [pltpu.VMEM((48, 128), F32)])
    return input_grad, gate_grad, up_grad, down_grad


def solution(mesh):
    fine = Mesh(mesh.devices.reshape(SIZES), AXES)
    row, col = ("z", "yh"), ("yl", "core")
    return jax.shard_map(
        on_device,
        mesh=fine,
        in_specs=(
            P(("depth",) + row, None),
            P(("depth",) + row, None),
            P("depth", row + col),
            P("depth", row + col),
            P(row + col, "depth"),
        ),
        out_specs=(
            P(("depth",) + row + col, None),
            P("depth", row + col),
            P("depth", row + col),
            P(row + col, "depth"),
        ),
        check_vma=False,
    )
```

```python
import jax
import jax.numpy as jnp
from jax import lax
from jax.experimental import pallas as pl
from jax.experimental.pallas import tpu as pltpu
from jax.sharding import Mesh
from jax.sharding import PartitionSpec as P

AXES = ("depth", "z", "yh", "yl", "core")
SIZES = (4, 8, 2, 2, 2)
BF16 = jnp.bfloat16
F32 = jnp.float32
HALF = 384
QUART = 192
GROUP = 96
WIDE = 2048
PART = 512
FF = 256
OTHERS = (2, 3, 1)


def exchange(x, axes):
    return lax.all_to_all(x, axes, split_axis=0, concat_axis=0, tiled=True)


def swap_core(x):
    return lax.ppermute(x, "core", [(0, 1), (1, 0)])


def swap_near(x):
    return lax.ppermute(x, "yl", [(0, 1), (1, 0)])


def swap_far(x):
    return lax.ppermute(x, ("yh", "yl"), [(0, 3), (3, 0), (1, 2), (2, 1)])


def swap_opposite(x):
    return lax.ppermute(x, "yh", [(0, 1), (1, 0)])


def swap_depth(x, k):
    return lax.ppermute(x, "depth", [(i, i ^ k) for i in range(4)])


def dot(left, right, dims):
    return lax.dot_general(left, right, (dims, ((), ())), preferred_element_type=F32)


def call(body, outs, args, flops, scratch=()):
    size = sum(a.size * a.dtype.itemsize for a in args)
    size += sum(o.size * o.dtype.itemsize for o in outs)
    vmem = pl.BlockSpec(memory_space=pltpu.VMEM)
    return list(pl.pallas_call(
        body,
        out_shape=outs,
        in_specs=[vmem] * len(args),
        out_specs=[vmem] * len(outs),
        scratch_shapes=list(scratch),
        compiler_params=pltpu.CompilerParams(vmem_limit_bytes=20 << 20),
        cost_estimate=pl.CostEstimate(flops=flops, bytes_accessed=size, transcendentals=0),
    )(*args))


def out(shape, dtype):
    return jax.ShapeDtypeStruct(shape, dtype)


def rows_of(k, size):
    return pl.ds(pl.multiple_of(k * size, size), size)


def column_parts():
    mine = lax.axis_index("core") * 2 + lax.axis_index("yl")
    return [rows_of(mine ^ k, PART) for k in range(4)]


def pack(tokens, out_grad, o, scr):
    mine = lax.axis_index("core") * 2 + lax.axis_index("yl")
    for kind, x in enumerate((tokens, out_grad)):
        for d in range(4):
            for c in range(4):
                lane = pl.multiple_of(mine * PART + d * WIDE + c * 128, 128)
                scr[pl.ds(c, 12, stride=4), :] = x[:, pl.ds(lane, 128)].astype(F32)
            block = scr[...].astype(BF16)
            for z in range(8):
                o[z * 4 + d, kind] = block


def unpack(came, lo_o, hi_o, scr):
    for kind in range(2):
        for i in range(32):
            scr[i * 48:(i + 1) * 48, :] = came[i, kind].astype(F32)
        for half, o in enumerate((lo_o, hi_o)):
            for t in range(6):
                for c in range(4):
                    block = scr[pl.ds((half * 6 + t) * 4 + c, 32, stride=48), :]
                    o[kind, t * 32:(t + 1) * 32, c * 128:(c + 1) * 128] = block.astype(BF16)


def forward(gate_w, up_w, down_w, *refs):
    xs, outs, scr = refs[:8], refs[8:12], refs[12]
    ps = column_parts()
    for half in range(2):
        rows = slice(half * QUART, (half + 1) * QUART)
        some = xs[half::2]
        for w, c in ((gate_w, 0), (up_w, FF)):
            scr[rows, c:c + FF] = sum(dot(x[0], w[p, :], ((1,), (0,))) for p, x in zip(ps, some))
        scr[rows, 2 * FF:] = sum(dot(x[1], down_w[:, p], ((1,), (1,))) for p, x in zip(ps, some))
    d = lax.axis_index("depth")
    for k, o in zip((0,) + OTHERS, outs):
        o[...] = scr[rows_of(d ^ k, GROUP), :].astype(o.dtype)


def grad_terms(p0, p1, p2, p3, *refs):
    terms_o, hidden_o = refs[-2:]
    total = sum(r[...].astype(F32) for r in (p0, p1, p2, p3))
    gate, up, hidden_grad = total[:, :FF], total[:, FF:2 * FF], total[:, 2 * FF:]
    sig = 1.0 / (1.0 + jnp.exp(-gate))
    act = gate * sig
    hidden = (act * up).astype(BF16)
    if len(refs) == 3:
        hidden_o[0] = refs[0][...]
        hidden_o[1] = hidden
    else:
        hidden_o[...] = hidden
    terms_o[:, :FF] = (hidden_grad * up * sig * (1.0 + gate * (1.0 - sig))).astype(BF16)
    terms_o[:, FF:] = (hidden_grad * act).astype(BF16)


def input_rows(terms, core, pick):
    yl = lax.axis_index("yl")
    for j in range(2):
        pick[j * GROUP:(j + 1) * GROUP, :] = terms[rows_of((yl ^ j) * 2 + core, GROUP), :]


def backward_other(t0, t1, t2, t3, gate_w, up_w, terms, o, pick):
    d = lax.axis_index("depth")
    for k, t in zip((0,) + OTHERS, (t0, t1, t2, t3)):
        terms[rows_of(d ^ k, GROUP), :] = t[...]
    input_rows(terms, 1 - lax.axis_index("core"), pick)
    for p in range(4):
        cols = slice(p * PART, (p + 1) * PART)
        total = dot(pick[:, :FF], gate_w[cols, :], ((1,), (1,)))
        total += dot(pick[:, FF:], up_w[cols, :], ((1,), (1,)))
        o[:, cols] = total.astype(BF16)


def backward_own(terms, gate_w, up_w, came, here, away, pick):
    input_rows(terms, lax.axis_index("core"), pick)
    for p in range(4):
        cols = slice(p * PART, (p + 1) * PART)
        total = dot(pick[:, :FF], gate_w[cols, :], ((1,), (1,)))
        total += dot(pick[:, FF:], up_w[cols, :], ((1,), (1,)))
        total += came[:, cols].astype(F32)
        here[:, cols] = total[:GROUP].astype(here.dtype)
        away[:, cols] = total[GROUP:].astype(away.dtype)


def sum_y(keep, near, far, opposite, o, scr):
    for r in range(3):
        for c in range(16):
            at = (slice(r * 32, (r + 1) * 32), slice(c * 128, (c + 1) * 128))
            total = keep[at] + near[at].astype(F32) + far[at].astype(F32) + opposite[at].astype(F32)
            scr[pl.ds(r * 16 + c, 32, stride=48), :] = total
    for i in range(32):
        o[i] = scr[i * 48:(i + 1) * 48, :].astype(BF16)


def sum_z(came, o, scr):
    for d in range(4):
        total = came[d].astype(F32)
        for z in range(1, 8):
            total = total + came[z * 4 + d].astype(F32)
        scr[...] = total
        for c in range(16):
            o[:, d * WIDE + c * 128:d * WIDE + (c + 1) * 128] = scr[pl.ds(c, 3, stride=16), :].astype(BF16)


def halves(refs):
    for i in range(4):
        yield i * QUART, refs[i // 2 * 8 + i % 2:i // 2 * 8 + 8:2]


def gate_up_grads(terms_a, terms_b, *refs):
    gate_o, up_o = refs[16:]
    for k, p in enumerate(column_parts()):
        total = 0.0
        for lo, xs in halves(refs):
            t = (terms_a, terms_b)[lo // HALF]
            total += dot(xs[k][0], t[lo % HALF:lo % HALF + QUART, :], ((0,), (0,)))
        gate_o[p, :] = total[:, :FF].astype(BF16)
        up_o[p, :] = total[:, FF:].astype(BF16)


def down_grads(h0, h1, h2, h3, *refs):
    o, hidden = refs[16:]
    d = lax.axis_index("depth")
    for k, h in enumerate((h0, h1, h2, h3)):
        for chunk in range(2):
            hidden[rows_of(chunk * 4 + (d ^ k), GROUP), :] = h[chunk]
    for k, p in enumerate(column_parts()):
        total = sum(dot(hidden[lo:lo + QUART, :], xs[k][1], ((0,), (0,))) for lo, xs in halves(refs))
        o[:, p] = total.astype(BF16)


def on_device(tokens, out_grad, gate_weight, up_weight, down_weight):
    block = out((2, QUART, PART), BF16)
    weights = [gate_weight, up_weight, down_weight]
    flops = HALF * 2048 * FF
    with jax.named_scope("slice_out"):
        (x,) = call(pack, [out((32, 2, 48, 128), BF16)], [tokens, out_grad], 0, [pltpu.VMEM((48, 128), F32)])
        x = exchange(x, ("z", "depth"))
        own = call(unpack, [block, block], [x], 0, [pltpu.VMEM((1536, 128), F32)])

    def forward_chunk(blocks):
        part = out((GROUP, 3 * FF), BF16)
        return call(
            forward, [out((GROUP, 3 * FF), F32), part, part, part], weights + blocks, 6 * flops,
            [pltpu.VMEM((HALF, 3 * FF), F32)])

    def sum_depth(parts):
        return [parts[0]] + [swap_depth(x, k) for x, k in zip(parts[1:], OTHERS)]

    def backward_in(terms):
        return call(
            backward_other, [out((HALF, 2 * FF), BF16), out((QUART, WIDE), BF16)],
            [terms] + [swap_depth(terms, k) for k in OTHERS] + weights[:2], 2 * flops,
            [pltpu.VMEM((QUART, 2 * FF), BF16)])

    def backward_out(terms, came, dtype):
        return call(
            backward_own, [out((GROUP, WIDE), dtype), out((GROUP, WIDE), BF16)],
            [terms] + weights[:2] + [came], 2 * flops, [pltpu.VMEM((QUART, 2 * FF), BF16)])

    with jax.named_scope("collect"):
        first = [swap_near(x) for x in own] + [swap_far(x) for x in own] + [swap_core(x) for x in own]
        first = lax.optimization_barrier(first)
        near, far, own_s = first[:2], first[2:4], first[4:]
        opposite = [swap_near(far[0]), swap_far(near[1])]
        block_a = own + near + own_s + [swap_core(x) for x in near]
        far_s = [swap_core(x) for x in far]
    with jax.named_scope("forward_a"):
        parts_a = sum_depth(forward_chunk(block_a))
        tied = lax.optimization_barrier((*opposite, parts_a[1]))
        opposite = list(tied[:2])
        parts_a[1], = tied[2:]
    with jax.named_scope("collect_b"):
        block_b = list(opposite) + far + [swap_core(x) for x in opposite] + far_s
    with jax.named_scope("forward_b"):
        parts_b = sum_depth(forward_chunk(block_b))
    with jax.named_scope("terms_a"):
        piece = [out((GROUP, 2 * FF), BF16), out((GROUP, FF), BF16)]
        terms_a, hidden = call(grad_terms, piece, parts_a, 20 * GROUP * FF)
    with jax.named_scope("terms_b"):
        piece = [out((GROUP, 2 * FF), BF16), out((2, GROUP, FF), BF16)]
        terms_b, hidden = call(grad_terms, piece, parts_b + [hidden], 20 * GROUP * FF)
    with jax.named_scope("backward_a"):
        terms_a, send = backward_in(terms_a)
        keep, near = backward_out(terms_a, swap_core(send), F32)
        near = swap_near(near)
    with jax.named_scope("backward_b"):
        terms_b, send = backward_in(terms_b)
        send, hidden = lax.optimization_barrier((send, hidden))
        opposite, far = backward_out(terms_b, swap_core(send), BF16)
        opposite, far = swap_opposite(opposite), swap_far(far)
    with jax.named_scope("gather_hidden"):
        hidden = [hidden] + [swap_depth(hidden, k) for k in (1, 2, 3)]
    with jax.named_scope("gate_up_grads"):
        weight = out((2048, FF), BF16)
        gate_grad, up_grad = call(
            gate_up_grads, [weight, weight], [terms_a, terms_b] + block_a + block_b, 8 * flops)
    with jax.named_scope("down_grads"):
        (down_grad,) = call(
            down_grads, [out((FF, 2048), BF16)], hidden + block_a + block_b, 4 * flops,
            [pltpu.VMEM((768, FF), BF16)])
    with jax.named_scope("reduce_z"):
        (x,) = call(
            sum_y, [out((32, 48, 128), BF16)], [keep, near, far, opposite], 3 * GROUP * WIDE,
            [pltpu.VMEM((1536, 128), F32)])
        x, gate_grad, up_grad, down_grad = lax.optimization_barrier((x, gate_grad, up_grad, down_grad))
        x = exchange(x, ("z", "depth"))
        (input_grad,) = call(sum_z, [out((3, 8192), BF16)], [x], 0, [pltpu.VMEM((48, 128), F32)])
    return input_grad, gate_grad, up_grad, down_grad


def solution(mesh):
    fine = Mesh(mesh.devices.reshape(SIZES), AXES)
    row, col = ("z", "yh"), ("yl", "core")
    return jax.shard_map(
        on_device,
        mesh=fine,
        in_specs=(
            P(("depth",) + row, None),
            P(("depth",) + row, None),
            P("depth", row + col),
            P("depth", row + col),
            P(row + col, "depth"),
        ),
        out_specs=(
            P(("depth",) + row + col, None),
            P("depth", row + col),
            P("depth", row + col),
            P(row + col, "depth"),
        ),
        check_vma=False,
    )
```

```python
import jax
import jax.numpy as jnp
from jax import lax
from jax.experimental import pallas as pl
from jax.experimental.pallas import tpu as pltpu
from jax.sharding import Mesh
from jax.sharding import PartitionSpec as P

AXES = ("depth", "z", "yh", "yl", "core")
SIZES = (4, 8, 2, 2, 2)
BF16 = jnp.bfloat16
F32 = jnp.float32
HALF = 384
QUART = 192
GROUP = 96
WIDE = 2048
PART = 512
FF = 256
OTHERS = (2, 3, 1)
TERMS_FROM = (2, 1, 3)


def exchange(x, axes):
    return lax.all_to_all(x, axes, split_axis=0, concat_axis=0, tiled=True)


def swap_core(x):
    return lax.ppermute(x, "core", [(0, 1), (1, 0)])


def swap_near(x):
    return lax.ppermute(x, "yl", [(0, 1), (1, 0)])


def swap_far(x):
    return lax.ppermute(x, ("yh", "yl"), [(0, 3), (3, 0), (1, 2), (2, 1)])


def swap_opposite(x):
    return lax.ppermute(x, "yh", [(0, 1), (1, 0)])


def swap_depth(x, k):
    return lax.ppermute(x, "depth", [(i, i ^ k) for i in range(4)])


def dot(left, right, dims):
    return lax.dot_general(left, right, (dims, ((), ())), preferred_element_type=F32)


def call(body, outs, args, flops, scratch=()):
    size = sum(a.size * a.dtype.itemsize for a in args)
    size += sum(o.size * o.dtype.itemsize for o in outs)
    vmem = pl.BlockSpec(memory_space=pltpu.VMEM)
    return list(pl.pallas_call(
        body,
        out_shape=outs,
        in_specs=[vmem] * len(args),
        out_specs=[vmem] * len(outs),
        scratch_shapes=list(scratch),
        compiler_params=pltpu.CompilerParams(vmem_limit_bytes=20 << 20),
        cost_estimate=pl.CostEstimate(flops=flops, bytes_accessed=size, transcendentals=0),
    )(*args))


def out(shape, dtype):
    return jax.ShapeDtypeStruct(shape, dtype)


def rows_of(k, size):
    return pl.ds(pl.multiple_of(k * size, size), size)


def column_parts():
    mine = lax.axis_index("core") * 2 + lax.axis_index("yl")
    return [rows_of(mine ^ k, PART) for k in range(4)]


def pack(tokens, out_grad, o, scr):
    mine = lax.axis_index("core") * 2 + lax.axis_index("yl")
    for kind, x in enumerate((tokens, out_grad)):
        for d in range(4):
            for c in range(4):
                lane = pl.multiple_of(mine * PART + d * WIDE + c * 128, 128)
                scr[pl.ds(c, 12, stride=4), :] = x[:, pl.ds(lane, 128)].astype(F32)
            block = scr[...].astype(BF16)
            for z in range(8):
                o[z * 4 + d, kind] = block


def unpack(came, lo_o, hi_o, scr):
    for kind in range(2):
        for i in range(32):
            scr[i * 48:(i + 1) * 48, :] = came[i, kind].astype(F32)
        for half, o in enumerate((lo_o, hi_o)):
            for t in range(6):
                for c in range(4):
                    block = scr[pl.ds((half * 6 + t) * 4 + c, 32, stride=48), :]
                    o[kind, t * 32:(t + 1) * 32, c * 128:(c + 1) * 128] = block.astype(BF16)


def forward(gate_w, up_w, down_w, *refs):
    xs, outs, scr = refs[:8], refs[8:12], refs[12]
    ps = column_parts()
    for half in range(2):
        rows = slice(half * QUART, (half + 1) * QUART)
        some = xs[half::2]
        for w, c in ((gate_w, 0), (up_w, FF)):
            scr[rows, c:c + FF] = sum(dot(x[0], w[p, :], ((1,), (0,))) for p, x in zip(ps, some))
        scr[rows, 2 * FF:] = sum(dot(x[1], down_w[:, p], ((1,), (1,))) for p, x in zip(ps, some))
    d = lax.axis_index("depth")
    for k, o in zip((0,) + OTHERS, outs):
        o[...] = scr[rows_of(d ^ k, GROUP), :].astype(o.dtype)


def grad_terms(p0, p1, p2, p3, *refs):
    terms_o, hidden_o = refs[-2:]
    total = sum(r[...].astype(F32) for r in (p0, p1, p2, p3))
    gate, up, hidden_grad = total[:, :FF], total[:, FF:2 * FF], total[:, 2 * FF:]
    sig = 1.0 / (1.0 + jnp.exp(-gate))
    act = gate * sig
    hidden = (act * up).astype(BF16)
    if len(refs) == 3:
        hidden_o[0] = refs[0][...]
        hidden_o[1] = hidden
    else:
        hidden_o[...] = hidden
    terms_o[:, :FF] = (hidden_grad * up * sig * (1.0 + gate * (1.0 - sig))).astype(BF16)
    terms_o[:, FF:] = (hidden_grad * act).astype(BF16)


def input_rows(terms, core, pick):
    yl = lax.axis_index("yl")
    for j in range(2):
        pick[j * GROUP:(j + 1) * GROUP, :] = terms[rows_of((yl ^ j) * 2 + core, GROUP), :]


def backward_other(t0, t1, t2, t3, gate_w, up_w, terms, o, pick):
    d = lax.axis_index("depth")
    for k, t in zip((0,) + TERMS_FROM, (t0, t1, t2, t3)):
        terms[rows_of(d ^ k, GROUP), :] = t[...]
    input_rows(terms, 1 - lax.axis_index("core"), pick)
    for p in range(4):
        cols = slice(p * PART, (p + 1) * PART)
        total = dot(pick[:, :FF], gate_w[cols, :], ((1,), (1,)))
        total += dot(pick[:, FF:], up_w[cols, :], ((1,), (1,)))
        o[:, cols] = total.astype(BF16)


def backward_own(terms, gate_w, up_w, came, here, away, pick):
    input_rows(terms, lax.axis_index("core"), pick)
    for p in range(4):
        cols = slice(p * PART, (p + 1) * PART)
        total = dot(pick[:, :FF], gate_w[cols, :], ((1,), (1,)))
        total += dot(pick[:, FF:], up_w[cols, :], ((1,), (1,)))
        total += came[:, cols].astype(F32)
        here[:, cols] = total[:GROUP].astype(here.dtype)
        away[:, cols] = total[GROUP:].astype(away.dtype)


def sum_y(keep, near, far, opposite, o, scr):
    for r in range(3):
        for c in range(16):
            at = (slice(r * 32, (r + 1) * 32), slice(c * 128, (c + 1) * 128))
            total = keep[at] + near[at].astype(F32) + far[at].astype(F32) + opposite[at].astype(F32)
            scr[pl.ds(r * 16 + c, 32, stride=48), :] = total
    for i in range(32):
        o[i] = scr[i * 48:(i + 1) * 48, :].astype(BF16)


def sum_z(came, o, scr):
    for d in range(4):
        total = came[d].astype(F32)
        for z in range(1, 8):
            total = total + came[z * 4 + d].astype(F32)
        scr[...] = total
        for c in range(16):
            o[:, d * WIDE + c * 128:d * WIDE + (c + 1) * 128] = scr[pl.ds(c, 3, stride=16), :].astype(BF16)


def halves(refs):
    for i in range(4):
        yield i * QUART, refs[i // 2 * 8 + i % 2:i // 2 * 8 + 8:2]


def gate_up_grads(terms_a, terms_b, *refs):
    gate_o, up_o = refs[16:]
    for k, p in enumerate(column_parts()):
        total = 0.0
        for lo, xs in halves(refs):
            t = (terms_a, terms_b)[lo // HALF]
            total += dot(xs[k][0], t[lo % HALF:lo % HALF + QUART, :], ((0,), (0,)))
        gate_o[p, :] = total[:, :FF].astype(BF16)
        up_o[p, :] = total[:, FF:].astype(BF16)


def down_grads(h0, h1, h2, h3, *refs):
    o, hidden = refs[16:]
    d = lax.axis_index("depth")
    for k, h in enumerate((h0, h1, h2, h3)):
        for chunk in range(2):
            hidden[rows_of(chunk * 4 + (d ^ k), GROUP), :] = h[chunk]
    for k, p in enumerate(column_parts()):
        total = sum(dot(hidden[lo:lo + QUART, :], xs[k][1], ((0,), (0,))) for lo, xs in halves(refs))
        o[:, p] = total.astype(BF16)


def on_device(tokens, out_grad, gate_weight, up_weight, down_weight):
    block = out((2, QUART, PART), BF16)
    weights = [gate_weight, up_weight, down_weight]
    flops = HALF * 2048 * FF
    with jax.named_scope("slice_out"):
        (x,) = call(pack, [out((32, 2, 48, 128), BF16)], [tokens, out_grad], 0, [pltpu.VMEM((48, 128), F32)])
        x = exchange(x, ("z", "depth"))
        own = call(unpack, [block, block], [x], 0, [pltpu.VMEM((1536, 128), F32)])

    def forward_chunk(blocks):
        part = out((GROUP, 3 * FF), BF16)
        return call(
            forward, [out((GROUP, 3 * FF), F32), part, part, part], weights + blocks, 6 * flops,
            [pltpu.VMEM((HALF, 3 * FF), F32)])

    def sum_depth(parts):
        return [parts[0]] + [swap_depth(x, k) for x, k in zip(parts[1:], OTHERS)]

    def backward_in(terms):
        return call(
            backward_other, [out((HALF, 2 * FF), BF16), out((QUART, WIDE), BF16)],
            [terms] + [swap_depth(terms, k) for k in TERMS_FROM] + weights[:2], 2 * flops,
            [pltpu.VMEM((QUART, 2 * FF), BF16)])

    def backward_out(terms, came, dtype):
        return call(
            backward_own, [out((GROUP, WIDE), dtype), out((GROUP, WIDE), BF16)],
            [terms] + weights[:2] + [came], 2 * flops, [pltpu.VMEM((QUART, 2 * FF), BF16)])

    with jax.named_scope("collect"):
        first = [swap_near(x) for x in own] + [swap_far(x) for x in own] + [swap_core(x) for x in own]
        first = lax.optimization_barrier(first)
        near, far, own_s = first[:2], first[2:4], first[4:]
        opposite = [swap_near(far[0]), swap_far(near[1])]
        block_a = own + near + own_s + [swap_core(x) for x in near]
        far_s = [swap_core(x) for x in far]
    with jax.named_scope("forward_a"):
        parts_a = sum_depth(forward_chunk(block_a))
        tied = lax.optimization_barrier((*opposite, parts_a[1]))
        opposite = list(tied[:2])
        parts_a[1], = tied[2:]
    with jax.named_scope("collect_b"):
        block_b = list(opposite) + far + [swap_core(x) for x in opposite] + far_s
    with jax.named_scope("forward_b"):
        parts_b = sum_depth(forward_chunk(block_b))
    with jax.named_scope("terms_a"):
        piece = [out((GROUP, 2 * FF), BF16), out((GROUP, FF), BF16)]
        terms_a, hidden = call(grad_terms, piece, parts_a, 20 * GROUP * FF)
    with jax.named_scope("terms_b"):
        piece = [out((GROUP, 2 * FF), BF16), out((2, GROUP, FF), BF16)]
        terms_b, hidden = call(grad_terms, piece, parts_b + [hidden], 20 * GROUP * FF)
    with jax.named_scope("backward_a"):
        terms_a, send = backward_in(terms_a)
        keep, near = backward_out(terms_a, swap_core(send), F32)
        near = swap_near(near)
    with jax.named_scope("backward_b"):
        terms_b, send = backward_in(terms_b)
        send, hidden = lax.optimization_barrier((send, hidden))
        opposite, far = backward_out(terms_b, swap_core(send), BF16)
        opposite, far = swap_opposite(opposite), swap_far(far)
    with jax.named_scope("gather_hidden"):
        hidden = [hidden] + [swap_depth(hidden, k) for k in (1, 2, 3)]
    with jax.named_scope("gate_up_grads"):
        weight = out((2048, FF), BF16)
        gate_grad, up_grad = call(
            gate_up_grads, [weight, weight], [terms_a, terms_b] + block_a + block_b, 8 * flops)
    with jax.named_scope("down_grads"):
        (down_grad,) = call(
            down_grads, [out((FF, 2048), BF16)], hidden + block_a + block_b, 4 * flops,
            [pltpu.VMEM((768, FF), BF16)])
    with jax.named_scope("reduce_z"):
        (x,) = call(
            sum_y, [out((32, 48, 128), BF16)], [keep, near, far, opposite], 3 * GROUP * WIDE,
            [pltpu.VMEM((1536, 128), F32)])
        x, gate_grad, up_grad, down_grad = lax.optimization_barrier((x, gate_grad, up_grad, down_grad))
        x = exchange(x, ("z", "depth"))
        (input_grad,) = call(sum_z, [out((3, 8192), BF16)], [x], 0, [pltpu.VMEM((48, 128), F32)])
    return input_grad, gate_grad, up_grad, down_grad


def solution(mesh):
    fine = Mesh(mesh.devices.reshape(SIZES), AXES)
    row, col = ("z", "yh"), ("yl", "core")
    return jax.shard_map(
        on_device,
        mesh=fine,
        in_specs=(
            P(("depth",) + row, None),
            P(("depth",) + row, None),
            P("depth", row + col),
            P("depth", row + col),
            P(row + col, "depth"),
        ),
        out_specs=(
            P(("depth",) + row + col, None),
            P("depth", row + col),
            P("depth", row + col),
            P(row + col, "depth"),
        ),
        check_vma=False,
    )
```
